128 devices in a mesh: dp: 4 (over y), expert: 32 (over x, z, core).
Axes of the slice: x: 4, y: 4, z: 4, core: 2. Of those that a mesh axis runs over, the one named last changes fastest.
Arguments:
- tokens: bfloat16 [16384, 2048], P(('dp', 'expert')), may hold values from -6 to 6
- cotangent: bfloat16 [16384, 2048], P(('dp', 'expert')), may hold values from -6 to 6
- expert_ids: int32 [16384, 6], P(('dp', 'expert')), may hold values from 0 to 31, as said below
- gate_fixed: int32 [16384, 6], P(('dp', 'expert')), may hold values from 1024 to 65535
- w_gate: bfloat16 [32, 2048, 704], P('expert'), may hold values from -0.125 to 0.125
- w_up: bfloat16 [32, 2048, 704], P('expert'), may hold values from -0.125 to 0.125
- w_down: bfloat16 [32, 704, 2048], P('expert'), may hold values from -0.21875 to 0.21875
Outputs:
- mixed: bfloat16 [16384, 2048], P(('dp', 'expert'))
- token_grad: bfloat16 [16384, 2048], P(('dp', 'expert'))
- grad_gate: float32 [32, 2048, 704], P('expert', 'dp')
- grad_up: float32 [32, 2048, 704], P('expert', 'dp')
- grad_down: float32 [32, 704, 2048], P('expert', None, 'dp')
The draws below stay inside these ranges and needn't reach their ends.
Inputs may be any that keep to these rules, and one draw needn't show every extreme that they name: `expert_ids`: each row names 6 different experts. Within the rows of one device (aligned blocks of 128 rows) no expert is named by more than 32 rows, and one expert, the same in every block, is named by exactly 32 rows.
All inputs are finite; a program needn't handle non-finite values.
Results may differ from the reference program's by a relative error of at most 0.0095.
Values may be sent and summed in bfloat16 or wider, within the bound.
A program may use at most 192 MiB of HBM per device.

```python
import jax
import jax.numpy as jnp
from jax import lax

D = 2048
FF = 704
TOP = 6
TOK_DEV = 128
EXPERTS = 32
CAP = 32
TOKENS = 16384
N_DP = 4
N_EXPERT = 32


def draw_expert_ids(key, part):
    block_count = TOKENS // TOK_DEV
    slot_total = TOK_DEV * TOP
    full_expert = jax.random.randint(jax.random.fold_in(key, 11), (), 0, EXPERTS)
    others = EXPERTS - 1
    rest_slots = slot_total - CAP
    base_load = rest_slots // others
    extra_count = rest_slots % others
    pair_count = others // 2

    def one_block(block_key):
        key_a, key_b, key_c, key_d = jax.random.split(block_key, 4)
        loads = base_load + (jnp.arange(others) < extra_count).astype(jnp.int32)
        loads = jax.random.permutation(key_a, loads)
        giver_load = loads[0:2 * pair_count:2]
        taker_load = loads[1:2 * pair_count:2]
        room_left = jnp.minimum(giver_load - 1, CAP - taker_load)
        moved_rows = jax.random.randint(key_b, (pair_count,), 0, room_left + 1)
        loads = loads.at[0:2 * pair_count:2].add(-moved_rows)
        loads = loads.at[1:2 * pair_count:2].add(moved_rows)
        expert_index = jnp.arange(EXPERTS)
        other_pos = jnp.clip(expert_index - (expert_index > full_expert).astype(jnp.int32), 0, others - 1)
        counts = jnp.where(expert_index == full_expert, CAP, loads[other_pos])
        run_order = jax.random.permutation(key_c, EXPERTS)
        run_ends = jnp.cumsum(counts[run_order])
        labels = run_order[jnp.sum((run_ends[None, :] <= jnp.arange(slot_total)[:, None]).astype(jnp.int32), axis=1)]
        table_rows = labels.reshape(TOP, TOK_DEV).T
        return table_rows[jax.random.permutation(key_d, TOK_DEV)]
    block_keys = jax.random.split(jax.random.fold_in(key, 23), block_count)
    return jax.vmap(one_block)(block_keys).reshape(TOKENS, TOP).astype(jnp.int32)


def plant(result, stream_key, low, top_value):
    spot = [jax.random.randint(jax.random.fold_in(stream_key, axis), (), 0, length) for axis, length in enumerate(result.shape)]
    main_axis = result.shape.index(max(result.shape))
    beside = spot[:main_axis] + [(spot[main_axis] + 1) % result.shape[main_axis]] + spot[main_axis + 1:]
    return result.at[tuple(spot)].set(low).at[tuple(beside)].set(top_value)


def levels(rng, shape, cuts, least, top_value):
    def one(dim, parts):
        heights = jax.random.uniform(jax.random.fold_in(jax.random.fold_in(rng, 6), dim), (parts,), jnp.float32, least / len(cuts), top_value / len(cuts))
        return jnp.repeat(jnp.exp(heights), shape[dim] // parts).reshape((-1,) + (1,) * (len(shape) - dim - 1))

    gain = one(*cuts[0])
    for cut in cuts[1:]:
        gain = gain * one(*cut)
    return gain


def centred(key, shape, width, limit, cuts=(), held_as=jnp.bfloat16):
    drawn = width * jax.random.normal(key, shape, jnp.float32)
    if cuts:
        drawn = drawn * levels(key, shape, cuts, -0.22, 0.18)
    return jnp.clip(drawn, -limit, limit).astype(held_as)


def setup_inputs(seed: int = 0) -> dict:
    streams_of = jax.random.split(jax.random.key(seed), 8)
    tokens = centred(streams_of[0], (TOKENS, D), 1.0, 6.0, ((0, 128),))
    cotangent = centred(streams_of[1], (TOKENS, D), 1.0, 6.0, ((0, 128),))
    expert_ids = draw_expert_ids(jax.random.fold_in(streams_of[7], 71), 0)
    gate_fixed = plant(jax.random.randint(streams_of[3], (TOKENS, TOP), 1024, 65536), jax.random.fold_in(streams_of[3], 1), 1024, 65535).astype(jnp.int32)
    w_gate = centred(streams_of[4], (EXPERTS, D, FF), D ** -0.5, 0.125, ((0, 32),))
    w_up = centred(streams_of[5], (EXPERTS, D, FF), D ** -0.5, 0.125, ((0, 32),))
    w_down = centred(streams_of[6], (EXPERTS, FF, D), FF ** -0.5, 0.21875, ((0, 32),))
    return {"tokens": tokens, "cotangent": cotangent, "expert_ids": expert_ids, "gate_fixed": gate_fixed, "w_gate": w_gate, "w_up": w_up, "w_down": w_down}


def reference(tokens, cotangent, expert_ids, gate_fixed, w_gate, w_up, w_down):
    flat_ids = expert_ids.reshape(-1)
    gate_values = gate_fixed.reshape(-1).astype(jnp.float32) / 65536.0
    max_rows = N_DP * N_EXPERT * CAP
    pair_total = TOKENS * TOP

    def per_expert(carry, expert_no):
        out_acc, grad_acc = carry
        matches = flat_ids == expert_no
        picked = jnp.nonzero(matches, size=max_rows, fill_value=pair_total)[0].astype(jnp.int32)
        is_valid = picked < pair_total
        safe_pick = jnp.where(is_valid, picked, 0).astype(jnp.int32)
        token_row = (safe_pick // TOP).astype(jnp.int32)
        rows_in = jnp.where(is_valid[:, None], tokens[token_row], jnp.zeros((), tokens.dtype))
        gate_rows = jnp.where(is_valid, gate_values[safe_pick], jnp.zeros((), jnp.float32))
        gate_w = w_gate[expert_no]
        up_w = w_up[expert_no]
        down_w = w_down[expert_no]
        gate_pre = jnp.dot(rows_in, gate_w, preferred_element_type=jnp.float32)
        up_pre = jnp.dot(rows_in, up_w, preferred_element_type=jnp.float32)
        sigma = jax.nn.sigmoid(gate_pre)
        activ = gate_pre * sigma
        hidden = (activ * up_pre).astype(jnp.bfloat16)
        expert_out = jnp.dot(hidden, down_w, preferred_element_type=jnp.float32).astype(jnp.bfloat16)
        dy_pair = (cotangent[token_row].astype(jnp.float32) * gate_rows[:, None]).astype(jnp.bfloat16)
        d_hidden = jnp.dot(dy_pair, down_w.T, preferred_element_type=jnp.float32)
        d_gate = (d_hidden * up_pre * (sigma * (1.0 + gate_pre * (1.0 - sigma)))).astype(jnp.bfloat16)
        d_up = (d_hidden * activ).astype(jnp.bfloat16)
        d_rows = (jnp.dot(d_gate, gate_w.T, preferred_element_type=jnp.float32)
                  + jnp.dot(d_up, up_w.T, preferred_element_type=jnp.float32)).astype(jnp.bfloat16)
        target = jnp.where(is_valid, token_row, TOKENS).astype(jnp.int32)
        out_acc = out_acc.at[target].add(gate_rows[:, None] * expert_out.astype(jnp.float32), mode="drop")
        grad_acc = grad_acc.at[target].add(d_rows.astype(jnp.float32), mode="drop")
        grad_gate = jnp.dot(rows_in.T, d_gate, preferred_element_type=jnp.float32)
        grad_up = jnp.dot(rows_in.T, d_up, preferred_element_type=jnp.float32)
        grad_down = jnp.dot(hidden.T, dy_pair, preferred_element_type=jnp.float32)
        return (out_acc, grad_acc), (grad_gate, grad_up, grad_down)

    start_carry = (jnp.zeros((TOKENS, D), jnp.float32), jnp.zeros((TOKENS, D), jnp.float32))
    (out_acc, grad_acc), (grad_gate, grad_up, grad_down) = lax.scan(
        per_expert, start_carry, jnp.arange(EXPERTS, dtype=jnp.int32))
    return (out_acc.astype(jnp.bfloat16), grad_acc.astype(jnp.bfloat16), grad_gate, grad_up, grad_down)
```

```python
import functools

import jax
import jax.numpy as jnp
from jax import lax
from jax.experimental import pallas as pl
from jax.experimental.pallas import tpu as pltpu
from jax.sharding import PartitionSpec as P

MESH = pl.DeviceIdType.MESH
CAP = 32
BF = jnp.bfloat16
F32 = jnp.float32


def dot_nn(a, b):
    return lax.dot_general(a, b, (((1,), (0,)), ((), ())), preferred_element_type=F32)


def dot_nt(a, b):
    return lax.dot_general(a, b, (((1,), (1,)), ((), ())), preferred_element_type=F32)


def dot_tn(a, b):
    return lax.dot_general(a, b, (((0,), (0,)), ((), ())), preferred_element_type=F32)


def layer(n, top, tab, tok, cot, wg, wu, wd, mixed, tgrad, gg, gu, gd, rs2,
          w, s1, tb, pb, pg, snd, rows, rel, prec, ownp, h_t, fa, fb, gs, rs1,
          in_sem, s1_s, s1_r, tb_s, tb_r, s2_s, s2_r, rt_s, rt_r, r1_s, r1_r,
          rs_s, rs_r, loc):
    tokens, width = tok.shape
    half = width // 2
    ff = w.shape[1]
    fh = ff // 2
    quart = width // 4
    blk = 2 * n * CAP
    slots = n * blk
    y = lax.axis_index("dp")
    e = lax.axis_index("expert")
    x = e // (2 * n)
    z = lax.rem(e // 2, n)
    c = lax.rem(e, 2)

    def dev(xx, zz, cc):
        return (y, xx * (2 * n) + zz * 2 + cc)

    def up(v, d):
        return lax.rem(v + d, n)

    def down(v, d):
        return lax.rem(v + n - d, n)

    def ring(hf, d):
        return dev(up(x, d), z, c) if hf == 0 else dev(x, up(z, d), c)

    def ring_back(hf, d):
        return dev(down(x, d), z, c) if hf == 0 else dev(x, down(z, d), c)

    y_up = lax.rem(y + 1, 4)
    y_dn = lax.rem(y + 3, 4)
    offsets = [(d, k) for d in range(n) for k in range(2) if (d, k) != (0, 0)]

    pltpu.make_async_copy(tab, tb.at[0, 0], in_sem.at[0]).start()
    pltpu.make_async_copy(tab, tb.at[1, 0], in_sem.at[1]).start()
    ins = []
    for t, src in enumerate((tok, cot)):
        for hf in range(2):
            cp = pltpu.make_async_copy(
                src.at[:, pl.ds(hf * half, half)], s1.at[t, hf, 0], in_sem.at[2 + 2 * t + hf])
            cp.start()
            ins.append(cp)
    wcp = []
    for i, src in enumerate((wg, wu, wd)):
        cp = pltpu.make_async_copy(src, w.at[i], in_sem.at[6 + i])
        cp.start()
        wcp.append(cp)

    bar = pltpu.get_barrier_semaphore()
    partners = []
    for d, k in offsets:
        partners.append(dev(x, up(z, d), lax.rem(c + k, 2)))
        if d > 0:
            partners.append(dev(up(x, d), z, lax.rem(c + k, 2)))
    partners.append((y_up, e))
    partners.append((y_dn, e))
    for p in partners:
        pl.semaphore_signal(bar, inc=1, device_id=p, device_id_type=MESH)
    pl.semaphore_wait(bar, len(partners))

    def remote(src, dst, s, r, d):
        return pltpu.make_async_remote_copy(
            src_ref=src, dst_ref=dst, send_sem=s, recv_sem=r, device_id=d, device_id_type=MESH)

    def tab_copy(hf, d):
        return remote(tb.at[hf, 0], tb.at[hf, d], tb_s.at[hf, d - 1], tb_r.at[hf, d - 1], ring(hf, d))

    def s1_copy(t, hf, d):
        return remote(s1.at[t, hf, 0], s1.at[t, hf, d], s1_s.at[t, hf, d - 1],
                      s1_r.at[t, hf, d - 1], ring(hf, d))

    pltpu.make_async_copy(tab, tb.at[0, 0], in_sem.at[0]).wait()
    pltpu.make_async_copy(tab, tb.at[1, 0], in_sem.at[1]).wait()
    for hf in range(2):
        for d in range(1, n):
            tab_copy(hf, d).start()
    for hf in range(2):
        ins[hf].wait()
        for d in range(1, n):
            s1_copy(0, hf, d).start()

    upper = (lax.broadcasted_iota(jnp.int32, (tokens, tokens), 0)
             < lax.broadcasted_iota(jnp.int32, (tokens, tokens), 1))
    upper = jnp.where(upper, 1.0, 0.0).astype(BF)
    row16 = lax.broadcasted_iota(jnp.int32, (16, tokens), 0)
    slot_no = lax.broadcasted_iota(jnp.int32, (CAP, tokens), 0).astype(F32)

    def make_p(hf, d):
        if hf == 0:
            names = x * (2 * n) + row16
        else:
            names = lax.shift_right_logical(row16, 1) * (2 * n) + z * 2 + lax.bitwise_and(row16, 1)
        table = tb[hf, d]
        hit = jnp.zeros((16, tokens), F32)
        gate = jnp.zeros((16, tokens), jnp.int32)
        for k in range(top):
            same = table[k:k + 1, :] == names
            hit = jnp.where(same, 1.0, hit)
            gate = jnp.where(same, table[8 + k:9 + k, :], gate)
        rank = dot_nn(hit.astype(BF), upper)
        rank = jnp.where(hit > 0.0, rank, -1.0)
        high = (lax.shift_right_logical(gate, 8) * 256).astype(F32)
        low = lax.bitwise_and(gate, 255).astype(F32)
        for i in range(2 * n):
            one = slot_no == rank[i:i + 1, :]
            at = pl.ds(i * CAP, CAP)
            pb[hf, d, at, :] = jnp.where(one, 1.0, 0.0).astype(BF)
            pg[hf, d, at, pl.ds(0, tokens)] = jnp.where(one, high[i:i + 1, :], 0.0).astype(BF)
            pg[hf, d, at, pl.ds(tokens, tokens)] = jnp.where(one, low[i:i + 1, :], 0.0).astype(BF)

    def relay_out(t, hf, d):
        at = down(x if hf == 0 else z, d)
        src = s1[t, hf, d]
        if t == 0:
            picked = dot_nn(pb[hf, d], src)
        else:
            picked = dot_nn(pg[hf, d], jnp.concatenate([src, src], axis=0)) * (1.0 / 65536.0)
        snd[t, hf, :, :, at] = picked.astype(BF).reshape(n, 2, CAP, half)

    for hf in range(2):
        make_p(hf, 0)
        relay_out(0, hf, 0)

    @pl.loop(1, n)
    def _(d):
        for hf in range(2):
            tab_copy(hf, d).wait()
            make_p(hf, d)

    @pl.loop(1, n)
    def _(d):
        for hf in range(2):
            s1_copy(0, hf, d).wait()

    for hf in range(2):
        ins[2 + hf].wait()
        for d in range(1, n):
            s1_copy(1, hf, d).start()

    @pl.loop(1, n)
    def _(d):
        for hf in range(2):
            relay_out(0, hf, d)

    def s2_copy(t, hf, d, k):
        j = 2 * d + k - 1
        cd = lax.rem(c + k, 2)
        if hf == 0:
            zd = up(z, d)
            return remote(snd.at[t, 0, zd, cd], rows.at[t, 0, z, c], s2_s.at[t, 0, j],
                          s2_r.at[t, 0, j], dev(x, zd, cd))
        xd = up(x, d)
        return remote(snd.at[t, 1, xd, cd], rows.at[t, 1, :, c, x], s2_s.at[t, 1, j],
                      s2_r.at[t, 1, j], dev(xd, z, cd))

    def s2_wait(t, hf, d, k):
        j = 2 * d + k - 1
        cf = lax.rem(c + k, 2)
        if hf == 0:
            land = rows.at[t, 0, down(z, d), cf]
        else:
            land = rows.at[t, 1, :, cf, down(x, d)]
        remote(land, land, s2_s.at[t, hf, j], s2_r.at[t, hf, j], dev(x, up(z, 1), c)).wait_recv()

    def s2_self(t, hf):
        if hf == 0:
            return pltpu.make_async_copy(snd.at[t, 0, z, c], rows.at[t, 0, z, c], loc.at[t, 0])
        return pltpu.make_async_copy(snd.at[t, 1, x, c], rows.at[t, 1, :, c, x], loc.at[t, 1])

    def s2_start(t):
        for d, k in offsets:
            for hf in range(2):
                s2_copy(t, hf, d, k).start()
        for hf in range(2):
            s2_self(t, hf).start()

    def s2_finish(t):
        for d, k in offsets:
            for hf in range(2):
                s2_wait(t, hf, d, k)
        for hf in range(2):
            s2_self(t, hf).wait()

    def s2_drain(t):
        for d, k in offsets:
            for hf in range(2):
                s2_copy(t, hf, d, k).wait_send()

    s2_start(0)
    for hf in range(2):
        relay_out(1, hf, 0)

    @pl.loop(1, n)
    def _(d):
        for hf in range(2):
            s1_copy(1, hf, d).wait()
            relay_out(1, hf, d)

    for cp in wcp:
        cp.wait()
    s2_finish(0)
    s2_start(1)
    s2_drain(0)

    @pl.loop(0, n)
    def _(b):
        cols = pl.ds(pl.multiple_of(b * blk, blk), blk)

        @pl.loop(0, 2)
        def _(f):
            part = pl.ds(pl.multiple_of(f * fh, fh), fh)
            xa = rows[0, 0, b].reshape(blk, half)
            xb = rows[0, 1, b].reshape(blk, half)
            gate = dot_nt(w[0, part, :half], xa) + dot_nt(w[0, part, half:], xb)
            upv = dot_nt(w[1, part, :half], xa) + dot_nt(w[1, part, half:], xb)
            s = jax.nn.sigmoid(gate)
            act = gate * s
            h_t[part, cols] = (act * upv).astype(BF)
            fa[part, cols] = (upv * (s * (1.0 + gate * (1.0 - s)))).astype(BF)
            fb[part, cols] = act.astype(BF)

        hid = h_t[:, cols]
        for hf in range(2):
            out = dot_tn(hid, w[2, :, hf * half:(hf + 1) * half])
            snd[0, hf, b] = out.astype(BF).reshape(2, n, CAP, half)

    def rt_copy(t, hf, d, k):
        j = 2 * d + k - 1
        cd = lax.rem(c + k, 2)
        if hf == 0:
            zd = up(z, d)
            return remote(snd.at[t, 0, zd, cd], rel.at[t, 0, z * 2 + c], rt_s.at[t, 0, j],
                          rt_r.at[t, 0, j], dev(x, zd, cd))
        xd = up(x, d)
        return remote(snd.at[t, 1, :, cd, xd], rel.at[t, 1, x * 2 + c], rt_s.at[t, 1, j],
                      rt_r.at[t, 1, j], dev(xd, z, cd))

    def rt_wait(t, hf, d, k):
        j = 2 * d + k - 1
        cf = lax.rem(c + k, 2)
        land = rel.at[t, hf, down(z if hf == 0 else x, d) * 2 + cf]
        remote(land, land, rt_s.at[t, hf, j], rt_r.at[t, hf, j], dev(x, up(z, 1), c)).wait_recv()

    def rt_self(t, hf):
        if hf == 0:
            return pltpu.make_async_copy(snd.at[t, 0, z, c], rel.at[t, 0, z * 2 + c], loc.at[2 + t, 0])
        return pltpu.make_async_copy(snd.at[t, 1, :, c, x], rel.at[t, 1, x * 2 + c], loc.at[2 + t, 1])

    def rt_start(t):
        for d, k in offsets:
            for hf in range(2):
                rt_copy(t, hf, d, k).start()
        for hf in range(2):
            rt_self(t, hf).start()

    def rt_finish(t):
        for d, k in offsets:
            for hf in range(2):
                rt_wait(t, hf, d, k)
        for hf in range(2):
            rt_self(t, hf).wait()

    def rt_drain(t):
        for d, k in offsets:
            for hf in range(2):
                rt_copy(t, hf, d, k).wait_send()

    rt_start(0)
    s2_finish(1)

    def quarter(i, left, t, q, f):
        part = pl.ds(pl.multiple_of(f * fh, fh), fh)
        cols = pl.ds(pl.multiple_of(lax.rem(q, 2) * quart, quart), quart)
        right = rows[t, q // 2, :, :, :, :, cols].reshape(slots, quart)
        return part, dot_nn(left[part, :], right)

    def rs_first(i, way):
        part = pl.ds(way * fh, fh)
        return remote(gs.at[i, 0, part], rs1.at[i, way], rs_s.at[i, way], rs_r.at[i, way],
                      (y_up if way == 0 else y_dn, e))

    def rs_second(i, way, f):
        part = pl.ds(f * fh, fh)
        j = 2 + 2 * way + f
        return remote(gs.at[i, 1 + way, part], rs2.at[i, way, part], rs_s.at[i, j], rs_r.at[i, j],
                      (y_up if way == 0 else y_dn, e))

    def grad_start(i, left, t, own):
        owners = (lax.rem(y + 2, 4), y_up, y_dn)
        for o in range(3):
            @pl.loop(0, 2)
            def _(f):
                part, val = quarter(i, left, t, owners[o], f)
                gs[i, o, part, :] = val.astype(BF)
            if o == 0:
                rs_first(i, 0).start()
                rs_first(i, 1).start()
            elif o == 1:
                rs_second(i, 0, 1).start()
            else:
                rs_second(i, 1, 0).start()

        @pl.loop(0, 2)
        def _(f):
            part, val = quarter(i, left, t, y, f)
            own[part, :] = val

    def grad_middle(i):
        for way in range(2):
            part = pl.ds(way * fh, fh)
            rs_first(i, way).wait()
            gs[i, 1 + way, part, :] = (
                gs[i, 1 + way, part, :].astype(F32) + rs1[i, way].astype(F32)).astype(BF)
            rs_second(i, way, way).start()

    def grad_finish(i, own):
        cps = []
        for way in range(2):
            for f in range(2):
                rs_second(i, way, f).wait()
            cp = pltpu.make_async_copy(rs2.at[i, way], gs.at[i, 1 + way], in_sem.at[way])
            cp.start()
            cps.append(cp)
        for cp in cps:
            cp.wait()

        @pl.loop(0, 2)
        def _(f):
            part = pl.ds(pl.multiple_of(f * fh, fh), fh)
            own[part, :] = own[part, :] + gs[i, 1, part, :].astype(F32) + gs[i, 2, part, :].astype(F32)

    grad_start(0, h_t, 1, gd)

    @pl.loop(0, n)
    def _(b):
        cols = pl.ds(pl.multiple_of(b * blk, blk), blk)

        @pl.loop(0, 2)
        def _(f):
            part = pl.ds(pl.multiple_of(f * fh, fh), fh)
            dh = (dot_nt(w[2, part, :half], rows[1, 0, b].reshape(blk, half))
                  + dot_nt(w[2, part, half:], rows[1, 1, b].reshape(blk, half)))
            fa[part, cols] = (dh * fa[part, cols].astype(F32)).astype(BF)
            fb[part, cols] = (dh * fb[part, cols].astype(F32)).astype(BF)

    grad_middle(0)
    s2_drain(1)

    @pl.loop(0, n)
    def _(b):
        cols = pl.ds(pl.multiple_of(b * blk, blk), blk)
        dg = fa[:, cols]
        du = fb[:, cols]
        for hf in range(2):
            span = slice(hf * half, (hf + 1) * half)
            out = dot_tn(dg, w[0, :, span]) + dot_tn(du, w[1, :, span])
            snd[1, hf, b] = out.astype(BF).reshape(2, n, CAP, half)

    rt_start(1)
    grad_start(1, fa, 0, gg)

    def r1_copy(t, hf, d):
        return remote(s1.at[t, hf, d], prec.at[t, hf, d - 1], r1_s.at[t, hf, d - 1],
                      r1_r.at[t, hf, d - 1], ring_back(hf, d))

    def relay_sum(t, hf, d):
        at = down(x if hf == 0 else z, d)
        got = rel[t, hf, :, at].reshape(blk, half)
        if t == 0:
            both = dot_tn(pg[hf, d], got)
            return (both[:tokens] + both[tokens:]) * (1.0 / 65536.0)
        return dot_tn(pb[hf, d], got)

    def relay_back(t):
        @pl.loop(1, n)
        def _(d):
            for hf in range(2):
                s1[t, hf, d] = relay_sum(t, hf, d).astype(BF)
                r1_copy(t, hf, d).start()

        for hf in range(2):
            ownp[hf] = relay_sum(t, hf, 0)

    def last_sum(t, out):
        for hf in range(2):
            total = ownp[hf]
            for d in range(1, n):
                r1_copy(t, hf, d).wait()
                total = total + prec[t, hf, d - 1].astype(F32)
            out[:, hf * half:(hf + 1) * half] = total.astype(BF)

    rt_finish(0)
    relay_back(0)
    grad_start(2, fb, 0, gu)
    grad_middle(1)
    last_sum(0, mixed)
    rt_finish(1)
    relay_back(1)
    grad_middle(2)
    grad_finish(0, gd)
    last_sum(1, tgrad)
    grad_finish(1, gg)
    grad_finish(2, gu)
    rt_drain(0)
    rt_drain(1)


def shards(n, tokens, cotangent, expert_ids, gate_fixed, w_gate, w_up, w_down):
    rows, width = tokens.shape
    top = expert_ids.shape[1]
    ff = w_down.shape[1]
    half = width // 2
    quart = width // 4
    pad = ((0, 8 - top), (0, 0))
    tab = jnp.concatenate(
        [jnp.pad(expert_ids.T, pad, constant_values=-1), jnp.pad(gate_fixed.T, pad)], axis=0)
    any_spec = pl.BlockSpec(memory_space=pl.ANY)
    vm = pl.BlockSpec(memory_space=pltpu.VMEM)
    dma = pltpu.SemaphoreType.DMA
    blk = 2 * n * CAP
    slots = n * blk
    big = (2, 2, n, 2, n, CAP, half)
    grad = jax.ShapeDtypeStruct((ff, quart), F32)
    act = jax.ShapeDtypeStruct((rows, width), BF)
    outs = pl.pallas_call(
        functools.partial(layer, n, top),
        out_shape=(act, act, grad, grad, grad, jax.ShapeDtypeStruct((3, 2, ff, quart), BF)),
        in_specs=[any_spec] * 6,
        out_specs=[vm] * 5 + [any_spec],
        scratch_shapes=[
            pltpu.VMEM((3, ff, width), BF),
            pltpu.VMEM((2, 2, n, rows, half), BF),
            pltpu.VMEM((2, n, 16, rows), jnp.int32),
            pltpu.VMEM((2, n, blk, rows), BF),
            pltpu.VMEM((2, n, blk, 2 * rows), BF),
            pltpu.VMEM(big, BF),
            pltpu.VMEM(big, BF),
            pltpu.VMEM((2, 2, 2 * n, n, CAP, half), BF),
            pltpu.VMEM((2, 2, n - 1, rows, half), BF),
            pltpu.VMEM((2, rows, half), F32),
            pltpu.VMEM((ff, slots), BF),
            pltpu.VMEM((ff, slots), BF),
            pltpu.VMEM((ff, slots), BF),
            pltpu.VMEM((3, 3, ff, quart), BF),
            pltpu.VMEM((3, 2, ff // 2, quart), BF),
            dma((9,)),
            dma((2, 2, n - 1)), dma((2, 2, n - 1)),
            dma((2, n - 1)), dma((2, n - 1)),
            dma((2, 2, 2 * n - 1)), dma((2, 2, 2 * n - 1)),
            dma((2, 2, 2 * n - 1)), dma((2, 2, 2 * n - 1)),
            dma((2, 2, n - 1)), dma((2, 2, n - 1)),
            dma((3, 6)), dma((3, 6)),
            dma((4, 2)),
        ],
        compiler_params=pltpu.CompilerParams(
            collective_id=0, has_side_effects=True, vmem_limit_bytes=67043328),
    )(tab, tokens, cotangent, w_gate[0].T, w_up[0].T, w_down[0])
    mixed, tgrad, gg, gu, gd = outs[:5]
    return (mixed, tgrad, gg.T[None], gu.T[None], gd[None])


def solution(mesh):
    n = round((mesh.shape["expert"] // 2) ** 0.5)
    in_specs = (
        P(("dp", "expert"), None),
        P(("dp", "expert"), None),
        P(("dp", "expert"), None),
        P(("dp", "expert"), None),
        P("expert", None, None),
        P("expert", None, None),
        P("expert", None, None),
    )
    out_specs = (
        P(("dp", "expert"), None),
        P(("dp", "expert"), None),
        P("expert", "dp", None),
        P("expert", "dp", None),
        P("expert", None, "dp"),
    )
    return jax.shard_map(functools.partial(shards, n), mesh=mesh, in_specs=in_specs,
                         out_specs=out_specs, check_vma=False)
```

```python
import functools

import jax
import jax.numpy as jnp
from jax import lax
from jax.experimental import pallas as pl
from jax.experimental.pallas import tpu as pltpu
from jax.sharding import PartitionSpec as P

MESH = pl.DeviceIdType.MESH
CAP = 32
N = 4
BF = jnp.bfloat16
F32 = jnp.float32


def dot_nn(a, b):
    return lax.dot_general(a, b, (((1,), (0,)), ((), ())), preferred_element_type=F32)


def dot_nt(a, b):
    return lax.dot_general(a, b, (((1,), (1,)), ((), ())), preferred_element_type=F32)


def dot_tn(a, b):
    return lax.dot_general(a, b, (((0,), (0,)), ((), ())), preferred_element_type=F32)


def layer(top, tab, tok, cot, wg, wu, wd, mixed, tgrad, own_out, rs2,
          w, s1, tb, pb, pg, snd, rows, rel, p1, p2, ownp, h_t, fa, fb, gs, rs1, own, mix, tgr,
          in_sem, s1_s, s1_r, tb_s, tb_r, s2_s, s2_r, rt_s, rt_r, r1_s, r1_r,
          rs_s, rs_r, loc, out_sem):
    n = N
    tokens, width = tok.shape
    half = width // 2
    th = tokens // 2
    ff = w.shape[2]
    fh = ff // 2
    quart = width // 4
    piece = width // 8
    blk = 2 * n * CAP
    slots = n * blk
    y = lax.axis_index("dp")
    e = lax.axis_index("expert")
    x = e // (2 * n)
    z = lax.rem(e // 2, n)
    c = lax.rem(e, 2)

    def dev(xx, zz, cc):
        return (y, xx * (2 * n) + zz * 2 + cc)

    def up(v, d):
        return lax.rem(v + d, n)

    def down(v, d):
        return lax.rem(v + n - d, n)

    def ring(hf, d):
        return dev(up(x, d), z, c) if hf == 0 else dev(x, up(z, d), c)

    y_up = lax.rem(y + 1, 4)
    y_dn = lax.rem(y + 3, 4)
    offsets = [(d, k) for d in range(n) for k in range(2) if (d, k) != (0, 0)]

    pltpu.make_async_copy(tab, tb.at[0, 0], in_sem.at[0]).start()
    pltpu.make_async_copy(tab, tb.at[1, 0], in_sem.at[1]).start()

    def columns(hf):
        for ab in range(2):
            for j in range(2):
                yield (pl.ds((2 * hf + j) * quart + ab * piece, piece),
                       pl.ds((2 * ab + j) * piece, piece))

    for t, src in enumerate((tok, cot)):
        for hf in range(2):
            for there, here in columns(hf):
                pltpu.make_async_copy(src.at[:, there], s1.at[t, hf, 0, :, here],
                                      in_sem.at[2 + 2 * t + hf]).start()
    for i, src in enumerate((wg, wu, wd)):
        for hf in range(2):
            for there, here in columns(hf):
                pltpu.make_async_copy(src.at[:, there], w.at[i, hf, :, here],
                                      in_sem.at[6 + 2 * i + hf]).start()

    def in_wait(t, hf):
        pltpu.make_async_copy(tok.at[:, pl.ds(0, half)], s1.at[t, hf, 0], in_sem.at[2 + 2 * t + hf]).wait()

    bar = pltpu.get_barrier_semaphore()
    partners = []
    for d, k in offsets:
        partners.append(dev(x, up(z, d), lax.rem(c + k, 2)))
        if d > 0:
            partners.append(dev(up(x, d), z, lax.rem(c + k, 2)))
    partners.append((y_up, e))
    partners.append((y_dn, e))
    for p in partners:
        pl.semaphore_signal(bar, inc=1, device_id=p, device_id_type=MESH)
    pl.semaphore_wait(bar, len(partners))

    def remote(src, dst, s, r, d):
        return pltpu.make_async_remote_copy(
            src_ref=src, dst_ref=dst, send_sem=s, recv_sem=r, device_id=d, device_id_type=MESH)

    def tab_copy(hf, d):
        return remote(tb.at[hf, 0], tb.at[hf, d], tb_s.at[hf, d - 1], tb_r.at[hf, d - 1], ring(hf, d))

    def s1_copy(t, hf, way):
        d = 1 if way == 0 else 3
        return remote(s1.at[t, hf, 0], s1.at[t, hf, d], s1_s.at[t, hf, way],
                      s1_r.at[t, hf, way], ring(hf, d))

    def s1_pass(t, hf, way):
        d = 1 if way == 0 else 3
        part = pl.ds(way * th, th)
        return remote(s1.at[t, hf, d, part], s1.at[t, hf, 2, part], s1_s.at[t, hf, 2 + way],
                      s1_r.at[t, hf, 2 + way], ring(hf, d))

    pltpu.make_async_copy(tab, tb.at[0, 0], in_sem.at[0]).wait()
    pltpu.make_async_copy(tab, tb.at[1, 0], in_sem.at[1]).wait()
    for hf in range(2):
        for d in range(1, n):
            tab_copy(hf, d).start()
    for t in range(2):
        for hf in range(2):
            in_wait(t, hf)
            for way in range(2):
                s1_copy(t, hf, way).start()

    upper = (lax.broadcasted_iota(jnp.int32, (tokens, tokens), 0)
             < lax.broadcasted_iota(jnp.int32, (tokens, tokens), 1))
    upper = jnp.where(upper, 1.0, 0.0).astype(BF)
    row16 = lax.broadcasted_iota(jnp.int32, (16, tokens), 0)
    slot_no = lax.broadcasted_iota(jnp.int32, (CAP, tokens), 0).astype(F32)

    def make_p(hf, d):
        if hf == 0:
            names = x * (2 * n) + row16
        else:
            names = lax.shift_right_logical(row16, 1) * (2 * n) + z * 2 + lax.bitwise_and(row16, 1)
        table = tb[hf, d]
        hit = jnp.zeros((16, tokens), F32)
        gate = jnp.zeros((16, tokens), jnp.int32)
        for k in range(top):
            same = table[k:k + 1, :] == names
            hit = jnp.where(same, 1.0, hit)
            gate = jnp.where(same, table[8 + k:9 + k, :], gate)
        rank = dot_nn(hit.astype(BF), upper)
        rank = jnp.where(hit > 0.0, rank, -1.0)
        high = (lax.shift_right_logical(gate, 8) * 256).astype(F32)
        low = lax.bitwise_and(gate, 255).astype(F32)
        for i in range(2 * n):
            one = slot_no == rank[i:i + 1, :]
            at = pl.ds(i * CAP, CAP)
            pb[hf, d, at, :] = jnp.where(one, 1.0, 0.0).astype(BF)
            pg[hf, d, at, pl.ds(0, tokens)] = jnp.where(one, high[i:i + 1, :], 0.0).astype(BF)
            pg[hf, d, at, pl.ds(tokens, tokens)] = jnp.where(one, low[i:i + 1, :], 0.0).astype(BF)

    def relay_out(t, hf, d):
        at = down(x if hf == 0 else z, d)
        src = s1[t, hf, d]
        if t == 0:
            picked = dot_nn(pb[hf, d], src)
        else:
            picked = dot_nn(pg[hf, d], jnp.concatenate([src, src], axis=0)) * (1.0 / 65536.0)
        snd[t, hf, :, :, at] = picked.astype(BF).reshape(n, 2, CAP, half)

    for hf in range(2):
        make_p(hf, 0)
        relay_out(0, hf, 0)

    @pl.loop(1, n)
    def _(d):
        for hf in range(2):
            tab_copy(hf, d).wait()
            make_p(hf, d)

    for hf in range(2):
        for way in range(2):
            s1_copy(0, hf, way).wait()
            s1_pass(0, hf, way).start()
    for hf in range(2):
        relay_out(0, hf, 1)
        relay_out(0, hf, 3)
    for hf in range(2):
        for way in range(2):
            s1_copy(1, hf, way).wait()
            s1_pass(1, hf, way).start()

    def s2_copy(u, hf, d, k):
        j = 2 * d + k - 1
        cd = lax.rem(c + k, 2)
        t = min(u, 1)
        cols = pl.ds(0, half) if u == 0 else pl.ds((u - 1) * quart, quart)
        if hf == 0:
            zd = up(z, d)
            return remote(snd.at[t, 0, zd, cd, :, :, cols], rows.at[t, 0, z, c, :, :, cols],
                          s2_s.at[u, 0, j], s2_r.at[u, 0, j], dev(x, zd, cd))
        xd = up(x, d)
        return remote(snd.at[t, 1, xd, cd, :, :, cols], rows.at[t, 1, :, c, x, :, cols],
                      s2_s.at[u, 1, j], s2_r.at[u, 1, j], dev(xd, z, cd))

    def s2_wait(u, hf, d, k):
        j = 2 * d + k - 1
        cf = lax.rem(c + k, 2)
        t = min(u, 1)
        cols = pl.ds(0, half) if u == 0 else pl.ds((u - 1) * quart, quart)
        if hf == 0:
            land = rows.at[t, 0, down(z, d), cf, :, :, cols]
        else:
            land = rows.at[t, 1, :, cf, down(x, d), :, cols]
        remote(land, land, s2_s.at[u, hf, j], s2_r.at[u, hf, j], dev(x, up(z, 1), c)).wait_recv()

    def s2_self(t, hf):
        if hf == 0:
            return pltpu.make_async_copy(snd.at[t, 0, z, c], rows.at[t, 0, z, c], loc.at[t, 0])
        return pltpu.make_async_copy(snd.at[t, 1, x, c], rows.at[t, 1, :, c, x], loc.at[t, 1])

    def s2_start(u):
        for d, k in offsets:
            for hf in range(2):
                s2_copy(u, hf, d, k).start()

    def s2_finish(u):
        for d, k in offsets:
            for hf in range(2):
                s2_wait(u, hf, d, k)

    def s2_drain(u):
        for d, k in offsets:
            for hf in range(2):
                s2_copy(u, hf, d, k).wait_send()

    for hf in range(2):
        for way in range(2):
            s1_pass(0, hf, way).wait()
        relay_out(0, hf, 2)
    s2_start(0)
    for hf in range(2):
        s2_self(0, hf).start()
    for hf in range(2):
        relay_out(1, hf, 0)
        relay_out(1, hf, 1)
        relay_out(1, hf, 3)
    for hf in range(2):
        for way in range(2):
            s1_pass(1, hf, way).wait()
        relay_out(1, hf, 2)
    s2_start(1)
    s2_start(2)
    for hf in range(2):
        s2_self(1, hf).start()

    for i, src in enumerate((wg, wu, wd)):
        for hf in range(2):
            pltpu.make_async_copy(src.at[:, pl.ds(0, half)], w.at[i, hf], in_sem.at[6 + 2 * i + hf]).wait()
    s2_finish(0)
    for hf in range(2):
        s2_self(0, hf).wait()

    @pl.loop(0, n)
    def _(b):
        cols = pl.ds(pl.multiple_of(b * blk, blk), blk)

        @pl.loop(0, 2)
        def _(f):
            part = pl.ds(pl.multiple_of(f * fh, fh), fh)
            xa = rows[0, 0, b].reshape(blk, half)
            xb = rows[0, 1, b].reshape(blk, half)
            gate = dot_nt(w[0, 0, part, :], xa) + dot_nt(w[0, 1, part, :], xb)
            upv = dot_nt(w[1, 0, part, :], xa) + dot_nt(w[1, 1, part, :], xb)
            s = jax.nn.sigmoid(gate)
            act = gate * s
            h_t[part, cols] = (act * upv).astype(BF)
            fa[part, cols] = (upv * (s * (1.0 + gate * (1.0 - s)))).astype(BF)
            fb[part, cols] = act.astype(BF)

    def quarter(left, t, ab, q, f):
        part = pl.ds(pl.multiple_of(f * fh, fh), fh)
        cols = pl.ds(pl.multiple_of(ab * quart + lax.rem(q, 2) * piece, piece), piece)
        right = rows[t, q // 2, :, :, :, :, cols].reshape(slots, piece)
        return part, dot_nn(left[part, :], right)

    def rs_first(i, ab, way):
        part = pl.ds(way * fh, fh)
        return remote(gs.at[i, ab, 0, part], rs1.at[i, ab, way], rs_s.at[i, ab, way],
                      rs_r.at[i, ab, way], (y_up if way == 0 else y_dn, e))

    def rs_second(i, ab, way, f):
        part = pl.ds(f * fh, fh)
        j = 2 + 2 * way + f
        return remote(gs.at[i, ab, 1 + way, part], rs2.at[i, ab, way, part], rs_s.at[i, ab, j],
                      rs_r.at[i, ab, j], (y_up if way == 0 else y_dn, e))

    def grad_send(i, ab, left, t):
        owners = (lax.rem(y + 2, 4), y_up, y_dn)
        for o in range(3):
            @pl.loop(0, 2)
            def _(f):
                part, val = quarter(left, t, ab, owners[o], f)
                gs[i, ab, o, part, :] = val.astype(BF)
            if o == 0:
                rs_first(i, ab, 0).start()
                rs_first(i, ab, 1).start()
            elif o == 1:
                rs_second(i, ab, 0, 1).start()
            else:
                rs_second(i, ab, 1, 0).start()

    def grad_own(i, ab, left, t):
        @pl.loop(0, 2)
        def _(f):
            part, val = quarter(left, t, ab, y, f)
            own[i, part, pl.ds(ab * piece, piece)] = val

    def grad_middle(i, ab):
        for way in range(2):
            part = pl.ds(way * fh, fh)
            rs_first(i, ab, way).wait()
            gs[i, ab, 1 + way, part, :] = (
                gs[i, ab, 1 + way, part, :].astype(F32) + rs1[i, ab, way].astype(F32)).astype(BF)
            rs_second(i, ab, way, way).start()

    def rs_wait(i, ab):
        for way in range(2):
            for f in range(2):
                rs_second(i, ab, way, f).wait()

    def grad_finish(i):
        def stage(ab, way):
            return pltpu.make_async_copy(rs2.at[i, ab, way], gs.at[i, ab, 1 + way], out_sem.at[2 * ab + way])

        for ab in range(2):
            rs_wait(i, ab)
            for way in range(2):
                stage(ab, way).start()
        for ab in range(2):
            for way in range(2):
                stage(ab, way).wait()

            @pl.loop(0, 2)
            def _(f):
                part = pl.ds(pl.multiple_of(f * fh, fh), fh)
                cols = pl.ds(ab * piece, piece)
                own[i, part, cols] = (own[i, part, cols] + gs[i, ab, 1, part, :].astype(F32)
                                      + gs[i, ab, 2, part, :].astype(F32))

    def own_copy(i):
        return pltpu.make_async_copy(own.at[i], own_out.at[i], out_sem.at[4 + i])

    s2_finish(1)
    for hf in range(2):
        s2_self(1, hf).wait()
    grad_send(0, 0, h_t, 1)
    s2_drain(0)

    @pl.loop(0, n)
    def _(b):
        hid = h_t[:, pl.ds(pl.multiple_of(b * blk, blk), blk)]
        for hf in range(2):
            snd[0, hf, b] = dot_tn(hid, w[2, hf]).astype(BF).reshape(2, n, CAP, half)

    def rt_copy(t, hf, d, k):
        j = 2 * d + k - 1
        cd = lax.rem(c + k, 2)
        if hf == 0:
            zd = up(z, d)
            return remote(snd.at[t, 0, zd, cd], rel.at[t, 0, z * 2 + c], rt_s.at[t, 0, j],
                          rt_r.at[t, 0, j], dev(x, zd, cd))
        xd = up(x, d)
        return remote(snd.at[t, 1, :, cd, xd], rel.at[t, 1, x * 2 + c], rt_s.at[t, 1, j],
                      rt_r.at[t, 1, j], dev(xd, z, cd))

    def rt_wait(t, hf, d, k):
        j = 2 * d + k - 1
        cf = lax.rem(c + k, 2)
        land = rel.at[t, hf, down(z if hf == 0 else x, d) * 2 + cf]
        remote(land, land, rt_s.at[t, hf, j], rt_r.at[t, hf, j], dev(x, up(z, 1), c)).wait_recv()

    def rt_self(t, hf):
        if hf == 0:
            return pltpu.make_async_copy(snd.at[t, 0, z, c], rel.at[t, 0, z * 2 + c], loc.at[2 + t, 0])
        return pltpu.make_async_copy(snd.at[t, 1, :, c, x], rel.at[t, 1, x * 2 + c], loc.at[2 + t, 1])

    def rt_start(t):
        for d, k in offsets:
            for hf in range(2):
                rt_copy(t, hf, d, k).start()
        for hf in range(2):
            rt_self(t, hf).start()

    def rt_finish(t):
        for d, k in offsets:
            for hf in range(2):
                rt_wait(t, hf, d, k)
        for hf in range(2):
            rt_self(t, hf).wait()

    def rt_drain(t):
        for d, k in offsets:
            for hf in range(2):
                rt_copy(t, hf, d, k).wait_send()

    rt_start(0)
    grad_middle(0, 0)
    s2_finish(2)
    grad_send(0, 1, h_t, 1)

    @pl.loop(0, n)
    def _(b):
        cols = pl.ds(pl.multiple_of(b * blk, blk), blk)

        @pl.loop(0, 2)
        def _(f):
            part = pl.ds(pl.multiple_of(f * fh, fh), fh)
            dh = (dot_nt(w[2, 0, part, :], rows[1, 0, b].reshape(blk, half))
                  + dot_nt(w[2, 1, part, :], rows[1, 1, b].reshape(blk, half)))
            fa[part, cols] = (dh * fa[part, cols].astype(F32)).astype(BF)
            fb[part, cols] = (dh * fb[part, cols].astype(F32)).astype(BF)

    grad_middle(0, 1)
    grad_send(1, 0, fa, 0)
    s2_drain(1)
    s2_drain(2)

    @pl.loop(0, n)
    def _(b):
        cols = pl.ds(pl.multiple_of(b * blk, blk), blk)
        dg = fa[:, cols]
        du = fb[:, cols]
        for hf in range(2):
            out = dot_tn(dg, w[0, hf]) + dot_tn(du, w[1, hf])
            snd[1, hf, b] = out.astype(BF).reshape(2, n, CAP, half)

    rt_start(1)
    grad_middle(1, 0)
    grad_send(1, 1, fa, 0)

    def r1_first(t, hf, way):
        part = pl.ds(way * th, th)
        return remote(s1.at[t, hf, 2, part], p1.at[t, hf, way], r1_s.at[t, hf, way],
                      r1_r.at[t, hf, way], ring(hf, 3 if way == 0 else 1))

    def r1_second(t, hf, way, f):
        part = pl.ds(f * th, th)
        j = 2 + 2 * way + f
        return remote(s1.at[t, hf, 1 if way == 0 else 3, part], p2.at[t, hf, way, part],
                      r1_s.at[t, hf, j], r1_r.at[t, hf, j], ring(hf, 3 if way == 0 else 1))

    def relay_sum(t, hf, d):
        at = down(x if hf == 0 else z, d)
        got = rel[t, hf, :, at].reshape(blk, half)
        if t == 0:
            both = dot_tn(pg[hf, d], got)
            return (both[:tokens] + both[tokens:]) * (1.0 / 65536.0)
        return dot_tn(pb[hf, d], got)

    def relay_back(t):
        for hf in range(2):
            s1[t, hf, 2] = relay_sum(t, hf, 2).astype(BF)
            for way in range(2):
                r1_first(t, hf, way).start()
        for hf in range(2):
            for way in range(2):
                d = 1 if way == 0 else 3
                s1[t, hf, d] = relay_sum(t, hf, d).astype(BF)
                r1_second(t, hf, way, 1 - way).start()

    def relay_own(t):
        for hf in range(2):
            ownp[hf] = relay_sum(t, hf, 0)

    def relay_middle(t):
        for hf in range(2):
            for way in range(2):
                d = 1 if way == 0 else 3
                part = pl.ds(way * th, th)
                r1_first(t, hf, way).wait()
                s1[t, hf, d, part, :] = (
                    s1[t, hf, d, part, :].astype(F32) + p1[t, hf, way].astype(F32)).astype(BF)
                r1_second(t, hf, way, way).start()

    def last_sum(t, out):
        for hf in range(2):
            for way in range(2):
                for f in range(2):
                    r1_second(t, hf, way, f).wait()
            total = (ownp[hf] + p2[t, hf, 0].astype(F32) + p2[t, hf, 1].astype(F32)).astype(BF)
            for ab in range(2):
                for j in range(2):
                    at = (2 * hf + j) * quart + ab * piece
                    src = (2 * ab + j) * piece
                    out[:, at:at + piece] = total[:, src:src + piece]

    grad_own(0, 0, h_t, 1)
    grad_own(0, 1, h_t, 1)
    rt_finish(0)
    relay_back(0)
    grad_middle(1, 1)
    grad_send(2, 0, fb, 0)
    relay_middle(0)
    relay_own(0)
    grad_middle(2, 0)
    grad_send(2, 1, fb, 0)
    for ab in range(2):
        grad_own(1, ab, fa, 0)
        grad_own(2, ab, fb, 0)
    own_copy(2).start()
    last_sum(0, mix)
    mixed_out = pltpu.make_async_copy(mix, mixed, out_sem.at[7])
    mixed_out.start()
    grad_middle(2, 1)
    grad_finish(0)
    own_copy(0).start()
    rt_finish(1)
    relay_back(1)
    relay_own(1)
    relay_middle(1)
    grad_finish(1)
    own_copy(1).start()
    last_sum(1, tgr)
    tgrad_out = pltpu.make_async_copy(tgr, tgrad, out_sem.at[8])
    tgrad_out.start()
    rt_drain(0)
    rt_drain(1)
    rs_wait(2, 0)
    rs_wait(2, 1)
    for i in range(3):
        own_copy(i).wait()
    mixed_out.wait()
    tgrad_out.wait()


def finish(mixed, tgrad, own, rs2, mixed_out, tgrad_out, gg, gu, gd):
    mixed_out[...] = mixed[...]
    tgrad_out[...] = tgrad[...]
    gd[...] = own[0]
    gg[...] = own[1]
    piece = rs2.shape[-1]
    for ab in range(2):
        cols = slice(ab * piece, (ab + 1) * piece)
        gu[:, cols] = own[2, :, cols] + rs2[0, ab, 0].astype(F32) + rs2[0, ab, 1].astype(F32)


def shards(tokens, cotangent, expert_ids, gate_fixed, w_gate, w_up, w_down):
    rows, width = tokens.shape
    top = expert_ids.shape[1]
    ff = w_down.shape[1]
    half = width // 2
    quart = width // 4
    pad = ((0, 8 - top), (0, 0))
    tab = jnp.concatenate(
        [jnp.pad(expert_ids.T, pad, constant_values=-1), jnp.pad(gate_fixed.T, pad)], axis=0)
    any_spec = pl.BlockSpec(memory_space=pl.ANY)
    dma = pltpu.SemaphoreType.DMA
    n = N
    blk = 2 * n * CAP
    slots = n * blk
    piece = width // 8
    big = (2, 2, n, 2, n, CAP, half)
    grad = jax.ShapeDtypeStruct((ff, quart), F32)
    act = jax.ShapeDtypeStruct((rows, width), BF)
    parts = pl.pallas_call(
        functools.partial(layer, top),
        out_shape=(act, act, jax.ShapeDtypeStruct((3, ff, quart), F32),
                   jax.ShapeDtypeStruct((3, 2, 2, ff, piece), BF)),
        in_specs=[any_spec] * 6,
        out_specs=[any_spec] * 4,
        scratch_shapes=[
            pltpu.VMEM((3, 2, ff, half), BF),
            pltpu.VMEM((2, 2, n, rows, half), BF),
            pltpu.VMEM((2, n, 16, rows), jnp.int32),
            pltpu.VMEM((2, n, blk, rows), BF),
            pltpu.VMEM((2, n, blk, 2 * rows), BF),
            pltpu.VMEM(big, BF),
            pltpu.VMEM(big, BF),
            pltpu.VMEM((2, 2, 2 * n, n, CAP, half), BF),
            pltpu.VMEM((2, 2, 2, rows // 2, half), BF),
            pltpu.VMEM((2, 2, 2, rows, half), BF),
            pltpu.VMEM((2, rows, half), F32),
            pltpu.VMEM((ff, slots), BF),
            pltpu.VMEM((ff, slots), BF),
            pltpu.VMEM((ff, slots), BF),
            pltpu.VMEM((3, 2, 3, ff, piece), BF),
            pltpu.VMEM((3, 2, 2, ff // 2, piece), BF),
            pltpu.VMEM((3, ff, quart), F32),
            pltpu.VMEM((rows, width), BF),
            pltpu.VMEM((rows, width), BF),
            dma((12,)),
            dma((2, 2, 4)), dma((2, 2, 4)),
            dma((2, n - 1)), dma((2, n - 1)),
            dma((3, 2, 2 * n - 1)), dma((3, 2, 2 * n - 1)),
            dma((2, 2, 2 * n - 1)), dma((2, 2, 2 * n - 1)),
            dma((2, 2, 6)), dma((2, 2, 6)),
            dma((3, 2, 6)), dma((3, 2, 6)),
            dma((4, 2)),
            dma((9,)),
        ],
        compiler_params=pltpu.CompilerParams(
            collective_id=0, has_side_effects=True, vmem_limit_bytes=67043328),
    )(tab, tokens, cotangent, w_gate[0].T, w_up[0].T, w_down[0])
    steps = 4
    fs = ff // steps
    act_spec = pl.BlockSpec((rows // steps, width), lambda i: (i, 0))
    grad_spec = pl.BlockSpec((fs, quart), lambda i: (i, 0))
    mixed, tgrad, gg, gu, gd = pl.pallas_call(
        finish,
        grid=(steps,),
        out_shape=(act, act, grad, grad, grad),
        in_specs=[act_spec, act_spec, pl.BlockSpec((3, fs, quart), lambda i: (0, i, 0)),
                  pl.BlockSpec((1, 2, 2, fs, piece), lambda i: (2, 0, 0, i, 0))],
        out_specs=[act_spec, act_spec, grad_spec, grad_spec, grad_spec],
    )(*parts)
    return (mixed, tgrad, gg.T[None], gu.T[None], gd[None])


def solution(mesh):
    in_specs = (
        P(("dp", "expert"), None),
        P(("dp", "expert"), None),
        P(("dp", "expert"), None),
        P(("dp", "expert"), None),
        P("expert", None, None),
        P("expert", None, None),
        P("expert", None, None),
    )
    out_specs = (
        P(("dp", "expert"), None),
        P(("dp", "expert"), None),
        P("expert", "dp", None),
        P("expert", "dp", None),
        P("expert", None, "dp"),
    )
    return jax.shard_map(shards, mesh=mesh, in_specs=in_specs,
                         out_specs=out_specs, check_vma=False)
```
